128 devices in a mesh: layer: 4 (over z_lo, core), row: 8 (over z_hi, y), col: 4 (over x).
Axes of the slice: x: 4, y: 4, z: 4 (z_hi: 2, z_lo: 2; z = z_hi * 2 + z_lo), core: 2. Of those that a mesh axis runs over, the one named last changes fastest.
Arguments:
- grad: bfloat16 [32768, 8192], P(('layer', 'row'), 'col'), parts along dimension 0, may hold values from -6 to 6
- error: bfloat16 [32768, 8192], P(('layer', 'row'), 'col'), parts along dimension 0, may hold values from -2 to 2
- left_old: bfloat16 [32768, 512], P(('layer', 'row')), parts along dimension 0, may hold values from -0.25 to 0.25
- right_old: bfloat16 [32768, 512], P(('layer', 'col')), parts along dimension 0, may hold values from -0.25 to 0.25
- first_old: float32 [2048, 512], P('layer'), parts along dimension 0, may hold values from -3 to 3
- second_old: float32 [2048, 512], P('layer'), parts along dimension 0, may hold values from 0.05 to 1
Outputs:
- error_new: bfloat16 [32768, 8192], P(('layer', 'row'), 'col'), parts along dimension 0
- first_moment: float32 [2048, 512], P('layer'), parts along dimension 0
- second_moment: float32 [2048, 512], P('layer'), parts along dimension 0
- update: float32 [2048, 512], P('layer'), parts along dimension 0
The draws below stay inside these ranges and needn't reach their ends.
There are 4 independent parts, one for each index of `layer`. The reference program is written for one: setup_inputs(seed, part) draws one part's arguments, and reference() takes and returns one part's arrays. A program takes and returns all parts, laid end to end along the dimension named above; each array names one. Nothing has to cross between parts.
All inputs are finite; a program needn't handle non-finite values.
Results may differ from the reference program's by a relative error of at most 0.0075.
Values may be sent and summed in bfloat16 or wider, within the bound.
No kernel may reach another device: no remote copies, remote signals or barrier semaphores. Data moves between devices by JAX's collectives and lax.ppermute only.
A program may use at most 128 MiB of HBM per device.

```python
import math
import jax
import jax.numpy as jnp
from jax import lax

M = 8192
N = 8192
R = 512


def shard_levels(stream_key, extent, cuts, smallest, top_value):
    loudness, own = 1.0, jax.random.fold_in(stream_key, 6)
    for position, blocks in cuts:
        steps = jnp.exp(jax.random.uniform(jax.random.fold_in(own, position), (blocks,), jnp.float32, smallest / len(cuts), top_value / len(cuts)))
        loudness = loudness * jnp.repeat(steps, extent[position] // blocks).reshape([-1 if axis == position else 1 for axis in range(len(extent))])
    return loudness


def noise(rng, dims, deviation, most, cuts=(), kind=jnp.bfloat16):
    drawn = deviation * jax.random.normal(rng, dims, jnp.float32)
    if cuts:
        drawn = drawn * shard_levels(rng, dims, cuts, -0.22, 0.18)
    return jnp.clip(drawn, -most, most).astype(kind)


def setup_inputs(seed: int = 0, part: int = 0) -> dict:
    splits = jax.random.split(jax.random.key(seed), 7)
    part_keys = jax.random.split(jax.random.fold_in(splits[6], part), 7)
    return {
        "grad": noise(part_keys[0], (M, N), 1.0, 6.0, ((0, 8), (1, 4))),
        "error": noise(part_keys[1], (M, N), 0.3, 2.0, ((0, 8), (1, 4))),
        "left_old": noise(part_keys[2], (M, R), R ** -0.5, 0.25, ((0, 8),)),
        "right_old": noise(part_keys[3], (N, R), R ** -0.5, 0.25, ((0, 4),)),
        "first_old": noise(part_keys[4], (R, R), 0.5, 3.0, (), jnp.float32),
        "second_old": jnp.clip(jnp.exp(jax.random.uniform(part_keys[5], (R, R), jnp.float32, math.log(0.05), math.log(1.0))), 0.05, 1.0),
    }


def orthonormal(image):
    gram = lax.dot_general(image, image, (((0,), (0,)), ((), ())), precision=lax.Precision.HIGHEST)
    factor = jnp.linalg.cholesky(gram)
    return jax.scipy.linalg.solve_triangular(factor, image.T, lower=True).T.astype(jnp.bfloat16)

def reference(grad, error, left_old, right_old, first_old, second_old):
    highest = lax.Precision.HIGHEST
    across = (((0,), (0,)), ((), ()))
    left_image = jnp.dot(grad.astype(jnp.float32), right_old.astype(jnp.float32), preferred_element_type=jnp.float32)
    left_basis = orthonormal(left_image)
    right_image = lax.dot_general(grad.astype(jnp.float32), left_basis.astype(jnp.float32), across, preferred_element_type=jnp.float32)
    right_basis = orthonormal(right_image)
    summed = grad.astype(jnp.float32) + error.astype(jnp.float32)
    accum = summed.astype(jnp.bfloat16)
    carried = jnp.dot(accum.astype(jnp.float32), right_basis.astype(jnp.float32), preferred_element_type=jnp.float32)
    core = lax.dot_general(left_basis.astype(jnp.float32), carried, across, precision=highest)
    turn_left = lax.dot_general(left_basis.astype(jnp.float32), left_old.astype(jnp.float32), across, preferred_element_type=jnp.float32)
    turn_right = lax.dot_general(right_basis.astype(jnp.float32), right_old.astype(jnp.float32), across, preferred_element_type=jnp.float32)
    lifted = jnp.dot(left_basis.astype(jnp.float32), core, precision=highest).astype(jnp.bfloat16)
    rebuilt = lax.dot_general(lifted.astype(jnp.float32), right_basis.astype(jnp.float32), (((1,), (1,)), ((), ())), preferred_element_type=jnp.float32)
    error_new = (summed - rebuilt).astype(jnp.bfloat16)
    first_turned = jnp.dot(jnp.dot(turn_left, first_old, precision=highest), turn_right.T, precision=highest)
    excess = jnp.maximum(second_old - first_old * first_old, 0.0)
    second_turned = jnp.dot(jnp.dot(turn_left * turn_left, excess, precision=highest), (turn_right * turn_right).T, precision=highest) + first_turned * first_turned
    first_moment = 0.9 * first_turned + 0.1 * core
    second_moment = 0.999 * second_turned + 0.001 * core * core
    update = first_moment / (jnp.sqrt(second_moment) + 0.01)
    return (error_new, first_moment, second_moment, update)
```

```python
import jax
import jax.numpy as jnp
from jax import lax
from jax.experimental import pallas as pl
from jax.experimental.pallas import tpu as pltpu
from jax.sharding import PartitionSpec as P

BLOCK = 128
HIGHEST = lax.Precision.HIGHEST
F32 = jnp.float32
BF16 = jnp.bfloat16


def contract(a, b, ca, cb, precision=None):
    return lax.dot_general(
        a, b, (((ca,), (cb,)), ((), ())), precision=precision, preferred_element_type=F32
    )


def split_pair(values):
    upper = values.astype(BF16)
    return upper, (values - upper.astype(F32)).astype(BF16)


def packed_index(i, j):
    return (i * (i + 1)) // 2 + j


def eliminate(tiles, out_ref):
    full = (8, BLOCK)
    lane = lax.broadcasted_iota(jnp.int32, full, 1)
    sub = lax.broadcasted_iota(jnp.int32, full, 0)
    count = len(tiles)
    for g in range(count):
        top = tiles[g]
        base = 8 * g
        cols = [jnp.broadcast_to(top[:, base + m : base + m + 1], full) for m in range(8)]
        s = {}
        for j in range(8):
            for i in range(j, 8):
                s[i, j] = jnp.broadcast_to(cols[j][i : i + 1, :], full)
        inside = (lane >= base) & (lane < base + 8)
        head = jnp.where(inside, (lane - base == sub).astype(F32), top)
        u = []
        r = []
        for j in range(8):
            r.append(lax.rsqrt(s[j, j]))
            for i in range(j + 1, 8):
                s[i, j] = s[i, j] * r[j]
            for m in range(j + 1, 8):
                for i in range(m, 8):
                    s[i, m] = s[i, m] - s[i, j] * s[m, j]
            row = jnp.broadcast_to(head[j : j + 1, :], full)
            for i in range(j):
                row = row - s[j, i] * u[i]
            u.append(row * r[j])
        done = u[0]
        for j in range(1, 8):
            done = jnp.where(sub == j, u[j], done)
        out_ref[pl.ds(base, 8), :] = jnp.where(lane <= sub + base, done, 0.0)
        if g + 1 < count:
            v = [None] * 8
            for j in range(7, -1, -1):
                acc = u[j]
                for i in range(j + 1, 8):
                    acc = acc - s[i, j] * v[i]
                v[j] = acc * r[j]
            for t in range(g + 1, count):
                old = tiles[t]
                p = [
                    jnp.broadcast_to(old[:, base + m : base + m + 1], full) * v[m]
                    for m in range(8)
                ]
                total = ((p[0] + p[1]) + (p[2] + p[3])) + ((p[4] + p[5]) + (p[6] + p[7]))
                tiles[t] = jnp.where(inside, 0.0, old) - total


def inverse_factor_kernel(packed_ref, out_ref, work, diag, inv):
    n = out_ref.shape[0] // BLOCK
    for i in range(n):
        for j in range(i + 1):
            at = packed_index(i, j) * BLOCK
            work[i * BLOCK : (i + 1) * BLOCK, j * BLOCK : (j + 1) * BLOCK] = packed_ref[
                at : at + BLOCK, :
            ]
    diag[...] = packed_ref[0:BLOCK, :]
    out_ref[...] = jnp.zeros_like(out_ref)
    rows = lax.broadcasted_iota(jnp.int32, (BLOCK, BLOCK), 0)
    lanes = lax.broadcasted_iota(jnp.int32, (BLOCK, BLOCK), 1)
    unit = jnp.where(rows == lanes, 1.0, 0.0)
    for k in range(n):
        out_ref[k * BLOCK : (k + 1) * BLOCK, k * BLOCK : (k + 1) * BLOCK] = unit

    def step(k, carry):
        eliminate([diag[8 * t : 8 * t + 8, :] for t in range(BLOCK // 8)], inv)
        for q in range(n):

            @pl.when(k == q)
            def _():
                lo, hi = q * BLOCK, (q + 1) * BLOCK
                x = contract(inv[...], out_ref[lo:hi, 0:hi], 1, 0, HIGHEST)
                out_ref[lo:hi, 0:hi] = x
                if q + 1 < n:
                    low = contract(work[hi:, lo:hi], inv[...], 1, 1, HIGHEST)
                    work[hi:, hi:] = work[hi:, hi:] - contract(low, low, 1, 1, HIGHEST)
                    out_ref[hi:, 0:hi] = out_ref[hi:, 0:hi] - contract(low, x, 1, 0, HIGHEST)
                    diag[...] = work[hi : hi + BLOCK, hi : hi + BLOCK]

        return carry

    lax.fori_loop(0, n, step, 0)


def inverse_factor(packed, n):
    return pl.pallas_call(
        inverse_factor_kernel,
        out_shape=jax.ShapeDtypeStruct((n, n), F32),
        in_specs=[pl.BlockSpec(memory_space=pltpu.VMEM)],
        out_specs=pl.BlockSpec(memory_space=pltpu.VMEM),
        scratch_shapes=[
            pltpu.VMEM((n, n), F32),
            pltpu.VMEM((BLOCK, BLOCK), F32),
            pltpu.VMEM((BLOCK, BLOCK), F32),
        ],
        compiler_params=pltpu.CompilerParams(vmem_limit_bytes=12 << 20),
        cost_estimate=pl.CostEstimate(
            flops=20_000_000_000, bytes_accessed=8 * n * n, transcendentals=n
        ),
        name="inverse_factor",
    )(packed)


def piece_gram_kernel(pieces_ref, sum_ref, low_ref, packed_ref):
    total = pieces_ref[0].astype(F32)
    for i in range(1, pieces_ref.shape[0]):
        total = total + pieces_ref[i].astype(F32)
    upper = total.astype(BF16)
    lower = (total - upper.astype(F32)).astype(BF16)
    sum_ref[...] = upper
    low_ref[...] = lower
    n = total.shape[1] // BLOCK
    for i in range(n):
        width = (i + 1) * BLOCK
        mine_u = upper[:, i * BLOCK : width]
        mine_l = lower[:, i * BLOCK : width]
        block = contract(mine_u, upper[:, :width], 0, 0)
        block = block + contract(mine_u, lower[:, :width], 0, 0)
        block = block + contract(mine_l, upper[:, :width], 0, 0)
        for j in range(i + 1):
            at = packed_index(i, j) * BLOCK
            packed_ref[at : at + BLOCK, :] = block[:, j * BLOCK : (j + 1) * BLOCK]


def piece_gram(pieces):
    count, rows, n = pieces.shape
    blocks = n // BLOCK
    packed = (blocks * (blocks + 1)) // 2
    return pl.pallas_call(
        piece_gram_kernel,
        out_shape=(
            jax.ShapeDtypeStruct((rows, n), BF16),
            jax.ShapeDtypeStruct((rows, n), BF16),
            jax.ShapeDtypeStruct((packed * BLOCK, BLOCK), F32),
        ),
        in_specs=[pl.BlockSpec(memory_space=pltpu.VMEM)],
        out_specs=(
            pl.BlockSpec(memory_space=pltpu.VMEM),
            pl.BlockSpec(memory_space=pltpu.VMEM),
            pl.BlockSpec(memory_space=pltpu.VMEM),
        ),
        compiler_params=pltpu.CompilerParams(vmem_limit_bytes=16 << 20),
        cost_estimate=pl.CostEstimate(
            flops=6 * rows * n * n, bytes_accessed=2 * count * rows * n, transcendentals=0
        ),
        name="piece_gram",
    )(pieces)


def exchange(pieces, axes):
    return lax.all_to_all(pieces, axes, 0, 0)


def gather_rows(values, axes, count):
    copies = jnp.broadcast_to(values[None], (count,) + values.shape)
    got = exchange(copies, axes)
    return got.reshape((count * values.shape[0],) + values.shape[1:])


def sum_all(values, axes, count):
    rows = values.shape[0] // count
    mine = exchange(values.reshape((count, rows) + values.shape[1:]), axes).sum(0)
    return gather_rows(mine, axes, count)


def per_device(grad, error, left_old, right_old, first_old, second_old):
    n_row, n_col = lax.axis_size("row"), lax.axis_size("col")
    both = ("row", "col")
    rank = right_old.shape[1]
    m_rows, n_rows = grad.shape
    m_piece, n_piece = m_rows // n_col, n_rows // n_row

    summed = grad.astype(F32) + error.astype(F32)
    accum = summed.astype(BF16)

    left_part = contract(grad, right_old, 1, 0).astype(BF16)
    left_pieces = exchange(left_part.reshape(n_col, m_piece, rank), "col")
    left_mine, left_mine_low, left_packed = piece_gram(left_pieces)
    left_gram = sum_all(left_packed, both, n_row * n_col)
    left_image = gather_rows(left_mine, "col", n_col)
    left_start = lax.axis_index("col") * m_piece
    left_prior = lax.dynamic_slice_in_dim(left_old, left_start, m_piece, 0)
    turn_left_part = contract(left_mine, left_prior, 0, 0) + contract(
        left_mine_low, left_prior, 0, 0
    )
    turn_left_raw = sum_all(turn_left_part, both, n_row * n_col)

    left_inv = inverse_factor(left_gram, rank)
    left_u, left_l = split_pair(left_inv)
    left_basis = (contract(left_image, left_u, 1, 1) + contract(left_image, left_l, 1, 1)).astype(
        BF16
    )

    right_part = contract(grad, left_basis, 0, 0).astype(BF16)
    right_pieces = exchange(right_part.reshape(n_row, n_piece, rank), "row")
    pulled = contract(accum, left_basis, 0, 0).astype(BF16)
    right_mine, right_mine_low, right_packed = piece_gram(right_pieces)
    right_gram = sum_all(right_packed, both, n_row * n_col)
    right_image = gather_rows(right_mine, "row", n_row)
    right_start = lax.axis_index("row") * n_piece
    right_prior = lax.dynamic_slice_in_dim(right_old, right_start, n_piece, 0)
    turn_right_part = contract(right_mine, right_prior, 0, 0) + contract(
        right_mine_low, right_prior, 0, 0
    )
    core_part = contract(pulled, right_image, 0, 0)
    both_raw = sum_all(
        jnp.concatenate([core_part, turn_right_part], axis=1), both, n_row * n_col
    )
    core_raw, turn_right_raw = both_raw[:, :rank], both_raw[:, rank:]

    right_inv = inverse_factor(right_gram, rank)
    right_u, right_l = split_pair(right_inv)
    right_basis = (
        contract(right_image, right_u, 1, 1) + contract(right_image, right_l, 1, 1)
    ).astype(BF16)
    core = contract(core_raw, right_inv, 1, 1, HIGHEST)
    core_u, core_l = split_pair(core)
    lifted = (contract(left_basis, core_u, 1, 0) + contract(left_basis, core_l, 1, 0)).astype(BF16)
    rebuilt = contract(lifted, right_basis, 1, 1)
    error_new = (grad.astype(F32) + error.astype(F32) - rebuilt).astype(BF16)

    turn_left = contract(left_inv, turn_left_raw, 1, 0, HIGHEST)
    turn_right = contract(right_inv, turn_right_raw, 1, 0, HIGHEST)
    excess = jnp.maximum(second_old - first_old * first_old, 0.0)
    first_half = contract(turn_left, first_old, 1, 0, HIGHEST)
    second_half = contract(turn_left * turn_left, excess, 1, 0, HIGHEST)
    first_turned = contract(first_half, turn_right, 1, 1, HIGHEST)
    second_turned = (
        contract(second_half, turn_right * turn_right, 1, 1, HIGHEST) + first_turned * first_turned
    )
    first_moment = 0.9 * first_turned + 0.1 * core
    second_moment = 0.999 * second_turned + 0.001 * core * core
    update = first_moment / (jnp.sqrt(second_moment) + 0.01)
    return (error_new, first_moment, second_moment, update)


def solution(mesh):
    return jax.shard_map(
        per_device,
        mesh=mesh,
        in_specs=(
            P(("layer", "row"), "col"),
            P(("layer", "row"), "col"),
            P(("layer", "row"), None),
            P(("layer", "col"), None),
            P("layer", None),
            P("layer", None),
        ),
        out_specs=(
            P(("layer", "row"), "col"),
            P("layer", None),
            P("layer", None),
            P("layer", None),
        ),
        check_vma=False,
    )
```
